32 devices in a mesh: grp: 2 (over core), fsdp: 4 (over y, x), tp: 4 (over z).
Axes of the slice: x: 2, y: 2, z: 4, core: 2. Of those that a mesh axis runs over, the one named last changes fastest.
Arguments:
- layer_input: bfloat16 [8192, 2048], P(('grp', 'fsdp', 'tp')), may hold values from -6 to 6
- cotangent: bfloat16 [8192, 2048], P(('grp', 'fsdp', 'tp')), may hold values from -6 to 6
- prompt_blocks: int32 [2, 8], P('grp'), may hold values from 0 to 7, each once within a row
- cont_lengths: int32 [8, 3], P(('grp', 'fsdp')), may hold values from 1 to 512, 768 in all within a row
- first_gain: bfloat16 [2048], P(('grp', 'fsdp')), may hold values from 0.5 to 1.5
- first_shift: bfloat16 [2048], P(('grp', 'fsdp')), may hold values from -3 to 3
- query_weight: bfloat16 [2048, 2048], P(('grp', 'fsdp'), 'tp'), may hold values from -0.125 to 0.125
- query_bias: bfloat16 [16, 128], P('tp', ('grp', 'fsdp')), may hold values from -3 to 3
- keyval_weight: bfloat16 [2048, 256], P(('grp', 'fsdp')), may hold values from -0.125 to 0.125
- value_bias: bfloat16 [128], P(('grp', 'fsdp')), may hold values from -3 to 3
- output_weight: bfloat16 [2048, 2048], P('tp', ('grp', 'fsdp')), may hold values from -4 to 4
- output_bias: bfloat16 [2048], P(('grp', 'fsdp')), may hold values from -3 to 3
- second_gain: bfloat16 [2048], P(('grp', 'fsdp')), may hold values from 0.5 to 1.5
- second_shift: bfloat16 [2048], P(('grp', 'fsdp')), may hold values from -3 to 3
- upward_weight: bfloat16 [2048, 8192], P(('grp', 'fsdp'), 'tp'), may hold values from -0.125 to 0.125
- upward_bias: bfloat16 [64, 128], P('tp', ('grp', 'fsdp')), may hold values from -3 to 3
- downward_weight: bfloat16 [8192, 2048], P('tp', ('grp', 'fsdp')), may hold values from -0.0625 to 0.0625
- downward_bias: bfloat16 [2048], P(('grp', 'fsdp')), may hold values from -3 to 3
Outputs:
- layer_output: bfloat16 [8192, 2048], P(('grp', 'fsdp', 'tp'))
- input_gradient: bfloat16 [8192, 2048], P(('grp', 'fsdp', 'tp'))
- first_gain_gradient: float32 [2048], P(('grp', 'fsdp'))
- first_shift_gradient: float32 [2048], P(('grp', 'fsdp'))
- query_weight_gradient: float32 [2048, 2048], P(('grp', 'fsdp'), 'tp')
- query_bias_gradient: float32 [16, 128], P('tp', ('grp', 'fsdp'))
- keyval_weight_gradient: float32 [2048, 256], P(('grp', 'fsdp'))
- value_bias_gradient: float32 [128], P(('grp', 'fsdp'))
- output_weight_gradient: float32 [2048, 2048], P('tp', ('grp', 'fsdp'))
- output_bias_gradient: float32 [2048], P(('grp', 'fsdp'))
- second_gain_gradient: float32 [2048], P(('grp', 'fsdp'))
- second_shift_gradient: float32 [2048], P(('grp', 'fsdp'))
- upward_weight_gradient: float32 [2048, 8192], P(('grp', 'fsdp'), 'tp')
- upward_bias_gradient: float32 [64, 128], P('tp', ('grp', 'fsdp'))
- downward_weight_gradient: float32 [8192, 2048], P('tp', ('grp', 'fsdp'))
- downward_bias_gradient: float32 [2048], P(('grp', 'fsdp'))
The draws below stay inside these ranges and needn't reach their ends.
Inputs may be any that keep to these rules, and one draw needn't show every extreme that they name: `prompt_blocks`: each row is a permutation of the 8 prompt blocks of one group: place f holds, in order, the blocks named at entries f * 2 to f * 2 + 1. `cont_lengths`: row g * 4 + f lists, in order, the lengths of the 3 continuations that fill the 768 continuation rows of place f of group g; they sum to 768, and the longest of each row is 512.
All inputs are finite; a program needn't handle non-finite values.
Results may differ from the reference program's by a relative error of at most 0.025.
Values may be sent and summed in bfloat16 or wider, within the bound.
No kernel may reach another device: no remote copies, remote signals or barrier semaphores. Data moves between devices by JAX's collectives and lax.ppermute only.
A program may use at most 128 MiB of HBM per device.

```python
import math
import jax
import jax.numpy as jnp
import numpy as np
from jax import lax

D = 2048
HEADS = 16
HD = 128
FF = 8192
PBLK = 128
PB_DEV = 2
CLEN = 512
NCONT = 3
CONT_DEV = 768
QB = 512
PR_DEV = 256
PROMPT = 1024
NPB = 8
GROUP = 4096
TOKENS = 8192
N_GRP = 2
N_FSDP = 4


def with_spikes(values, key, source, target, shards_of, factor):
    def block_of(axis_at):
        return (jnp.arange(values.shape[axis_at]) // (values.shape[axis_at] // shards_of)).reshape((-1,) + (1,) * (values.ndim - 1 - axis_at))

    one_side = jax.random.permutation(key, shards_of)[block_of(target)]
    far = (block_of(target) + shards_of // 2) % shards_of
    return jnp.where((block_of(source) == one_side) | (block_of(source) == far), factor * values, values)


def block_levels(own_key, dims, cuts, least, top_value):
    level, own = 1.0, jax.random.fold_in(own_key, 6)
    for position, blocks in cuts:
        steps = jnp.exp(jax.random.uniform(jax.random.fold_in(own, position), (blocks,), jnp.float32, least / len(cuts), top_value / len(cuts)))
        level = level * jnp.repeat(steps, dims[position] // blocks).reshape([-1 if axis == position else 1 for axis in range(len(dims))])
    return level


def length_profile(number_of, total, reach, lean):
    weights = [(1 << 20) // math.isqrt(grade ** lean) + 1 for grade in range(2, number_of + 1)]
    rest, given = total - reach - (number_of - 1), [1] * (number_of - 1)
    while rest > 0:
        candidates = [i for i in range(number_of - 1) if given[i] < reach]
        mass, budget = sum([weights[i] for i in candidates]), rest
        for i in candidates:
            addition = min(reach - given[i], max(1, budget * weights[i] // mass), rest)
            given[i] = given[i] + addition
            rest = rest - addition
    return np.array([reach] + given)


def ragged(rng, amount, total, reach, slope):
    if amount == 2:
        one = jax.random.randint(rng, (), max(1, total - reach), min(reach, total - 1) + 1)
        return jnp.stack([one, total - one])
    sizes = jnp.asarray(length_profile(amount, total, reach, slope), jnp.int32)
    twos = (amount - 1) // 2
    giver, sink = sizes[1:1 + 2 * twos:2], sizes[2:2 + 2 * twos:2]
    slack = jnp.minimum(giver - 1, reach - sink)
    moved = jax.random.randint(jax.random.fold_in(rng, 1), (twos,), 0, 1 << 20) % (slack + 1)
    sizes = sizes.at[1:1 + 2 * twos:2].set(giver - moved).at[2:2 + 2 * twos:2].set(sink + moved)
    return sizes[jax.random.permutation(jax.random.fold_in(rng, 2), amount)]


def normal_values(own_key, extent, deviation, reach, split=(), kind=jnp.bfloat16):
    drawn = jax.random.normal(own_key, extent, jnp.float32) * deviation
    if len(split) > 0:
        drawn = block_levels(own_key, extent, split, -0.22, 0.18) * drawn
    return jnp.clip(drawn, min=-reach, max=reach).astype(kind)


def noise_with(stream_key, dims, scale, limit, cuts, heavy, held_as=jnp.bfloat16):
    array = scale * jax.random.normal(stream_key, dims, jnp.float32)
    if cuts:
        array = array * block_levels(stream_key, dims, cuts, -0.22, 0.18)
    return jnp.clip(with_spikes(array, jax.random.fold_in(stream_key, 3), *heavy), -limit, limit).astype(held_as)


def setup_inputs(seed: int = 0) -> dict:
    arg_keys = jax.random.split(jax.random.key(seed), 19)
    layer_input = normal_values(arg_keys[0], (TOKENS, D), 1.0, 6.0, ((0, 32),))
    cotangent = noise_with(arg_keys[1], (TOKENS, D), 1.0, 6.0, ((0, 32),), (0, 1, 32, 2.75))
    prompt_blocks = jax.vmap(lambda own: jax.random.permutation(own, NPB))(jax.random.split(arg_keys[2], N_GRP)).reshape((N_GRP, NPB)).astype(jnp.int32)
    cont_lengths = jax.vmap(lambda own: ragged(own, NCONT, CONT_DEV, CLEN, 2))(jax.random.split(arg_keys[3], (N_GRP * N_FSDP))).reshape((N_GRP * N_FSDP, NCONT)).astype(jnp.int32)
    first_gain = jnp.clip(1.0 + 0.1 * jax.random.normal(arg_keys[4], (D,), jnp.float32), 0.5, 1.5).astype(jnp.bfloat16)
    first_shift = normal_values(arg_keys[5], (D,), 0.3, 3.0, ((0, 8),))
    query_weight = normal_values(arg_keys[6], (D, D), D ** -0.5, 0.125, ((0, 8), (1, 4)))
    query_bias = normal_values(arg_keys[7], (HEADS, HD), 0.3, 3.0, ((0, 4), (1, 8)))
    keyval_weight = normal_values(arg_keys[8], (D, 2 * HD), D ** -0.5, 0.125, ((0, 8),))
    value_bias = normal_values(arg_keys[9], (HD,), 0.5, 3.0, ((0, 8),))
    output_weight = normal_values(arg_keys[10], (D, D), (max(1, 2 * D // (PROMPT + CONT_DEV))) ** -0.5, 4.0, ((0, 4), (1, 8)))
    output_bias = normal_values(arg_keys[11], (D,), 0.3, 3.0, ((0, 8),))
    second_gain = jnp.clip(1.0 + 0.1 * jax.random.normal(arg_keys[12], (D,), jnp.float32), 0.5, 1.5).astype(jnp.bfloat16)
    second_shift = normal_values(arg_keys[13], (D,), 0.3, 3.0, ((0, 8),))
    upward_weight = normal_values(arg_keys[14], (D, FF), D ** -0.5, 0.125, ((0, 8), (1, 4)))
    upward_bias = normal_values(arg_keys[15], (FF // HD, HD), 0.5, 3.0, ((0, 4), (1, 8)))
    downward_weight = normal_values(arg_keys[16], (FF, D), FF ** -0.5, 0.0625, ((0, 4), (1, 8)))
    downward_bias = normal_values(arg_keys[17], (D,), 0.3, 3.0, ((0, 8),))
    return dict(layer_input=layer_input, cotangent=cotangent, prompt_blocks=prompt_blocks, cont_lengths=cont_lengths, first_gain=first_gain, first_shift=first_shift, query_weight=query_weight, query_bias=query_bias, keyval_weight=keyval_weight, value_bias=value_bias, output_weight=output_weight, output_bias=output_bias, second_gain=second_gain, second_shift=second_shift, upward_weight=upward_weight, upward_bias=upward_bias, downward_weight=downward_weight, downward_bias=downward_bias)


@jax.custom_vjp
def low(v):
    return lax.optimization_barrier(v.astype(jnp.bfloat16)).astype(jnp.float32)

@jax.custom_vjp
def low_back(v):
    return v

def low_keep(v):
    return (low(v), None)

def low_pass(kept, grad):
    return (grad,)

def back_keep(v):
    return (v, None)

def back_low(kept, grad):
    return (low(grad),)
low.defvjp(low_keep, low_pass)
low_back.defvjp(back_keep, back_low)
EPSILON = 1e-05
MASKED = -1e+30
GELU_SLOPE = 0.7978845608028654
GELU_CUBIC = 0.044715

def matmul(left, right):
    return jnp.dot(left, right, precision=lax.Precision.HIGHEST, preferred_element_type=jnp.float32)

def layer_norm(values, gain, shift):
    centre = lax.optimization_barrier(jnp.mean(values, axis=-1, keepdims=True))
    centred = values - centre
    spread = lax.optimization_barrier(jnp.mean(centred * centred, axis=-1, keepdims=True))
    return centred * lax.rsqrt(spread + EPSILON) * gain + shift

def gelu_tanh(values):
    return 0.5 * values * (1.0 + jnp.tanh(GELU_SLOPE * (values + GELU_CUBIC * values * values * values)))

def labels(blocks, lengths):
    offsets = jnp.arange(PR_DEV, dtype=jnp.int32)
    owned = blocks.reshape(N_FSDP, PB_DEV)
    prompt_order = owned[:, offsets // PBLK] * PBLK + (offsets % PBLK)[None, :]
    spots = jnp.arange(CONT_DEV, dtype=jnp.int32)
    ends = jnp.cumsum(lengths, axis=1).astype(jnp.int32)
    segment = lax.optimization_barrier(jnp.sum((spots[None, :, None] >= ends[:, None, :]).astype(jnp.int32), axis=2)).astype(jnp.int32)
    places = jnp.arange(N_FSDP, dtype=jnp.int32)[:, None]
    cont_order = jnp.broadcast_to(PROMPT + spots[None, :], (N_FSDP, CONT_DEV)).astype(jnp.int32)
    order = jnp.concatenate([prompt_order.astype(jnp.int32), cont_order], axis=1).reshape(-1)
    owner = jnp.concatenate([jnp.full((N_FSDP, PR_DEV), -1, jnp.int32), (places * NCONT + segment).astype(jnp.int32)], axis=1).reshape(-1)
    return (order, owner)

def attend_group(queries, keyval, order, owner):
    keys = keyval[:, :HD]
    values = keyval[:, HD:]
    scale = HD ** (-0.5)

    def block(inputs):
        query_block, order_block, owner_block = inputs
        raw = low_back(jnp.einsum('qhd,kd->hqk', query_block, keys, precision=lax.Precision.HIGHEST) * scale)
        allowed = (order[None, :] <= order_block[:, None]) & ((owner[None, :] < 0) | (owner[None, :] == owner_block[:, None]))
        scores = jnp.where(allowed[None], raw, MASKED)
        top = lax.optimization_barrier(jnp.max(scores, axis=2, keepdims=True))
        weights = jnp.exp(scores - top)
        shares = weights / lax.optimization_barrier(jnp.sum(weights, axis=2, keepdims=True))
        return jnp.einsum('hqk,kd->qhd', low(shares), values, precision=lax.Precision.HIGHEST)
    count = GROUP // QB
    result = lax.map(jax.checkpoint(block), (queries.reshape(count, QB, HEADS, HD), order.reshape(count, QB), owner.reshape(count, QB)))
    return result.reshape(GROUP, HEADS * HD)

def forward(stream, first_gain, first_shift, query_weight, query_bias, keyval_weight, value_bias, output_weight, output_bias, second_gain, second_shift, upward_weight, upward_bias, downward_weight, downward_bias, orders, owners):
    normed = low(layer_norm(stream, first_gain, first_shift))
    queries = low_back(low(matmul(normed, query_weight) + query_bias.reshape(-1)))
    value_pad = jnp.concatenate([jnp.zeros((HD,), jnp.float32), value_bias])
    keyval = low_back(low(matmul(normed, keyval_weight) + value_pad))
    pieces = []
    for group in range(N_GRP):
        begin = group * GROUP
        pieces.append(attend_group(queries[begin:begin + GROUP], keyval[begin:begin + GROUP], orders[group], owners[group]))
    attended = low_back(low(jnp.concatenate(pieces, axis=0)))
    middle = stream + low_back(matmul(attended, output_weight)) + output_bias
    normed_two = low(layer_norm(middle, second_gain, second_shift))
    hidden = low_back(matmul(normed_two, upward_weight) + upward_bias.reshape(-1))
    active = low(gelu_tanh(hidden))
    return middle + matmul(active, downward_weight) + downward_bias

def reference(layer_input, cotangent, prompt_blocks, cont_lengths, first_gain, first_shift, query_weight, query_bias, keyval_weight, value_bias, output_weight, output_bias, second_gain, second_shift, upward_weight, upward_bias, downward_weight, downward_bias):
    orders = []
    owners = []
    for group in range(N_GRP):
        order, owner = labels(prompt_blocks[group], cont_lengths[group * N_FSDP:(group + 1) * N_FSDP])
        orders.append(order)
        owners.append(owner)
    params = (first_gain, first_shift, query_weight, query_bias, keyval_weight, value_bias, output_weight, output_bias, second_gain, second_shift, upward_weight, upward_bias, downward_weight, downward_bias)
    params = tuple((item.astype(jnp.float32) for item in params))

    def apply(stream, *weights):
        return forward(stream, *weights, orders, owners)
    output, pullback = jax.vjp(apply, layer_input.astype(jnp.float32), *params)
    grads = pullback(cotangent.astype(jnp.float32))
    return (output.astype(jnp.bfloat16), grads[0].astype(jnp.bfloat16), grads[1], grads[2], grads[3], grads[4], grads[5], grads[6], grads[7], grads[8], grads[9], grads[10], grads[11], grads[12], grads[13], grads[14])
```

```python
import jax
import jax.numpy as jnp
from jax import lax
from jax.sharding import PartitionSpec as P

HD = 128
PBLK = 128
PB_DEV = 2
CONT_DEV = 768
PR_DEV = 256
ROWS = 1024
HEAD_BLOCK = 4

EPSILON = 1e-05
MASKED = -1e30
GELU_SLOPE = 0.7978845608028654
GELU_CUBIC = 0.044715
GF = ("grp", "fsdp")
F32 = jnp.float32
BF16 = jnp.bfloat16


def layer_norm(values, gain, shift):
    centre = jnp.mean(values, axis=-1, keepdims=True)
    centred = values - centre
    spread = jnp.mean(centred * centred, axis=-1, keepdims=True)
    return centred * lax.rsqrt(spread + EPSILON) * gain + shift


def gelu_tanh(values):
    return (
        0.5
        * values
        * (1.0 + jnp.tanh(GELU_SLOPE * (values + GELU_CUBIC * values * values * values)))
    )


def visible(order_query, owner_query, order_key, owner_key):
    earlier = order_key[None, :] <= order_query[:, None]
    shared = (owner_key[None, :] < 0) | (owner_key[None, :] == owner_query[:, None])
    return earlier & shared


def dot(left, right):
    return jnp.dot(left, right, preferred_element_type=F32)


def shift(values, axis="tp"):
    count = lax.axis_size(axis)
    return lax.ppermute(values, axis, [(i, (i + 1) % count) for i in range(count)])


def flip(values, axis, step):
    count = lax.axis_size(axis)
    return lax.ppermute(values, axis, [(i, i ^ step) for i in range(count)])


def after(values, *others):
    return lax.optimization_barrier((values, *others))[0]


def ring_gather(values):
    blocks = [values]
    for _ in range(lax.axis_size("tp") - 1):
        blocks.append(shift(blocks[-1]))
    return blocks


def ring_place(blocks, axis):
    count = len(blocks)
    me = lax.axis_index("tp")
    width = blocks[0].shape[axis]
    shape = list(blocks[0].shape)
    shape[axis] = width * count
    whole = jnp.zeros(shape, blocks[0].dtype)
    for s, block in enumerate(blocks):
        whole = lax.dynamic_update_slice_in_dim(
            whole, block, lax.rem(me - s + count, count) * width, axis
        )
    return whole


def ring_scatter(parts):
    count = len(parts)
    total = parts[1 % count]
    for s in range(1, count):
        total = shift(total.astype(BF16)).astype(F32) + parts[(s + 1) % count]
    return total


def ring_parts(values, axis):
    count = lax.axis_size("tp")
    me = lax.axis_index("tp")
    width = values.shape[axis] // count
    return [
        lax.dynamic_slice_in_dim(values, lax.rem(me - s + count, count) * width, width, axis)
        for s in range(count)
    ]


def relative_gather(values):
    blocks = [values]
    for m in range(1, lax.axis_size("fsdp")):
        top = 1 << (m.bit_length() - 1)
        blocks.append(flip(blocks[m ^ top], "fsdp", top))
    return blocks


def halve(values, axis):
    step = lax.axis_size(axis)
    while step > 1:
        step //= 2
        half = values.shape[0] // 2
        values = values[:half] + flip(values[half:].astype(BF16), axis, step).astype(F32)
    return values


def total_over(values, axis):
    step = lax.axis_size(axis)
    while step > 1:
        step //= 2
        values = values + flip(values.astype(BF16), axis, step).astype(F32)
    return values


def on_device(
    layer_input,
    cotangent,
    prompt_blocks,
    cont_lengths,
    first_gain,
    first_shift,
    query_weight,
    query_bias,
    keyval_weight,
    value_bias,
    output_weight,
    output_bias,
    second_gain,
    second_shift,
    upward_weight,
    upward_bias,
    downward_weight,
    downward_bias,
):
    tp = lax.axis_size("tp")
    fsdp = lax.axis_size("fsdp")
    shards = lax.axis_size("grp") * fsdp
    place = lax.axis_index("fsdp")
    column = lax.axis_index("tp")
    owner_of = lax.axis_index("grp") * fsdp + place
    local_count, width = layer_input.shape
    heads_local = query_bias.shape[0]
    heads = heads_local * tp
    scale = HD ** (-0.5)

    query_rows = ring_place(ring_gather(query_weight), 1)
    output_rows = ring_place(ring_gather(output_weight), 0)
    cotangent_blocks = ring_gather(after(cotangent, query_rows, output_rows))

    pieces = [
        keyval_weight.reshape(-1),
        first_gain,
        first_shift,
        output_bias,
        second_gain,
        second_shift,
        downward_bias,
        query_bias.reshape(-1),
        value_bias,
        upward_bias.reshape(-1),
    ]
    sizes = [piece.shape[0] for piece in pieces]
    filled = sum(sizes)
    padded = -(-filled // 4096) * 4096
    packed = jnp.concatenate(pieces + [jnp.zeros((padded - filled,), BF16)])
    packed = lax.all_gather(packed.reshape(-1, 256), GF, axis=0, tiled=True)
    packed = packed.reshape(shards, padded)
    fields = []
    start = 0
    for size in sizes:
        fields.append(packed[:, start : start + size])
        start += size
    keyval_full = fields[0].reshape(width, 2 * HD)
    gain_one, shift_one, output_shift, gain_two, shift_two, downward_shift = (
        field.reshape(-1).astype(F32) for field in fields[1:7]
    )
    query_shift = (
        fields[7].reshape(shards, heads_local, -1).transpose(1, 0, 2).reshape(heads_local * HD)
    )
    query_shift = ring_place(ring_gather(query_shift), 0).astype(F32)
    value_shift = fields[8].reshape(-1).astype(F32)
    upward_shift = (
        fields[9]
        .reshape(shards, upward_bias.shape[0], -1)
        .transpose(1, 0, 2)
        .reshape(-1)
        .astype(F32)
    )

    query_full = lax.all_gather(query_rows, GF, axis=0, tiled=True)
    output_full = lax.all_gather(output_rows, GF, axis=1, tiled=True)
    upward_full = lax.all_gather(upward_weight, GF, axis=0, tiled=True)
    downward_full = lax.all_gather(downward_weight, GF, axis=1, tiled=True)

    blocks = prompt_blocks[0]
    prompt_total = blocks.shape[0] * PBLK
    offsets = jnp.arange(PBLK, dtype=jnp.int32)

    def order_of(spot):
        mine = lax.dynamic_slice_in_dim(blocks, spot * PB_DEV, PB_DEV)
        return (mine[:, None] * PBLK + offsets[None, :]).reshape(-1)

    prompt_order = jnp.concatenate([order_of(place ^ m) for m in range(fsdp)])
    spots = jnp.arange(CONT_DEV, dtype=jnp.int32)
    ends = jnp.cumsum(cont_lengths[0])
    segment = jnp.sum((spots[:, None] >= ends[None, :]).astype(jnp.int32), axis=1)
    cont_order = prompt_total + spots
    order_key = jnp.concatenate([prompt_order, cont_order])
    owner_key = jnp.concatenate([jnp.full((prompt_total,), -1, jnp.int32), segment])
    order_rows = jnp.concatenate([order_of(place), cont_order])
    owner_rows = jnp.concatenate([jnp.full((PR_DEV,), -1, jnp.int32), segment])
    order_query = lax.dynamic_slice_in_dim(order_rows, column * local_count, local_count)
    owner_query = lax.dynamic_slice_in_dim(owner_rows, column * local_count, local_count)
    allowed = visible(order_query, owner_query, order_key, owner_key)

    local_rows = layer_input.astype(F32)
    normed_wide, norm_one_back = jax.vjp(layer_norm, local_rows, gain_one, shift_one)
    normed = normed_wide.astype(BF16)
    value_pad = jnp.concatenate([jnp.zeros((HD,), F32), value_shift])
    keyval = (dot(normed, keyval_full) + value_pad).astype(BF16)
    place_keyval = ring_place(ring_gather(keyval), 0)
    all_keyval = jnp.concatenate(
        relative_gather(place_keyval[:PR_DEV]) + [place_keyval[PR_DEV:]], axis=0
    )
    keys = all_keyval[:, :HD]
    values = all_keyval[:, HD:]
    queries = (dot(normed, query_full) + query_shift).astype(BF16)
    head_blocks = heads // HEAD_BLOCK

    def by_heads(rows):
        return rows.reshape(local_count, head_blocks, HEAD_BLOCK, HD).transpose(1, 2, 0, 3)

    def by_rows(split):
        return split.transpose(2, 0, 1, 3).reshape(local_count, heads * HD)

    query_blocks = by_heads(queries)

    def attend_block(query_block):
        scores = jnp.einsum("hqd,kd->hqk", query_block, keys, preferred_element_type=F32) * scale
        scores = jnp.where(allowed[None], scores, MASKED)
        top = jnp.max(scores, axis=2, keepdims=True)
        weights = jnp.exp(scores - top)
        total = jnp.sum(weights, axis=2, keepdims=True)
        shares = (weights / total).astype(BF16)
        result = jnp.einsum("hqk,kd->hqd", shares, values, preferred_element_type=F32)
        return (result.astype(BF16), (top + jnp.log(total))[:, :, 0])

    attended_blocks, log_totals = lax.map(attend_block, query_blocks)
    attended = by_rows(attended_blocks)
    middle = local_rows + dot(attended, output_full) + output_shift
    normed_two_wide, norm_two_back = jax.vjp(layer_norm, middle, gain_two, shift_two)
    normed_two_blocks = ring_gather(normed_two_wide.astype(BF16))

    feed_parts = []
    back_parts = []
    active_blocks = []
    hidden_gradient_blocks = []
    for block, upstream_block in zip(normed_two_blocks, cotangent_blocks):
        hidden = dot(block, upward_full) + upward_shift
        active_wide, gelu_back = jax.vjp(gelu_tanh, hidden)
        active = active_wide.astype(BF16)
        active_gradient = dot(upstream_block, downward_full.T)
        hidden_gradient = gelu_back(active_gradient)[0].astype(BF16)
        active_blocks.append(active)
        hidden_gradient_blocks.append(hidden_gradient)
        back_parts.append(dot(hidden_gradient, upward_full.T))
        feed_parts.append(dot(active, downward_full))
    normed_two_gradient = ring_scatter(back_parts)
    feed_parts = lax.optimization_barrier((feed_parts, normed_two_gradient))[0]
    fed = ring_scatter(feed_parts)
    layer_output = (middle + fed + downward_shift).astype(BF16)

    upstream = cotangent.astype(F32)
    active_rows = jnp.concatenate(active_blocks, axis=0)
    upstream_rows = jnp.concatenate(cotangent_blocks, axis=0)
    normed_two_rows = jnp.concatenate(normed_two_blocks, axis=0)
    hidden_gradient_rows = jnp.concatenate(hidden_gradient_blocks, axis=0)
    downward_gradient = lax.psum_scatter(
        dot(active_rows.T, upstream_rows).astype(BF16), GF, scatter_dimension=1, tiled=True
    ).astype(F32)
    upward_gradient = lax.psum_scatter(
        dot(normed_two_rows.T, hidden_gradient_rows).astype(BF16),
        GF,
        scatter_dimension=0,
        tiled=True,
    ).astype(F32)
    upward_shift_gradient = jnp.sum(hidden_gradient_rows, axis=0, dtype=F32)
    downward_shift_gradient = jnp.sum(upstream, axis=0)

    middle_part, gain_two_gradient, shift_two_gradient = norm_two_back(normed_two_gradient)
    middle_gradient = upstream + middle_part
    output_shift_gradient = jnp.sum(middle_gradient, axis=0)
    mixed_gradient = middle_gradient.astype(BF16)
    attended_gradient = dot(mixed_gradient, output_full.T).astype(BF16)
    output_sum = lax.psum_scatter(
        dot(attended.T, mixed_gradient).astype(BF16), GF, scatter_dimension=1, tiled=True
    ).astype(F32)
    output_gradient = ring_scatter(ring_parts(output_sum, 0))

    def back_block(carry, inputs):
        query_block, gradient_block, log_block = inputs
        scores = jnp.einsum("hqd,kd->hqk", query_block, keys, preferred_element_type=F32) * scale
        scores = jnp.where(allowed[None], scores, MASKED)
        shares = jnp.exp(scores - log_block[:, :, None])
        share_gradient = jnp.einsum(
            "hqd,kd->hqk", gradient_block, values, preferred_element_type=F32
        )
        centre = jnp.sum(share_gradient * shares, axis=2, keepdims=True)
        score_gradient = (shares * (share_gradient - centre)).astype(BF16)
        query_gradient = (
            jnp.einsum("hqk,kd->hqd", score_gradient, keys, preferred_element_type=F32) * scale
        )
        key_gradient = (
            jnp.einsum("hqk,hqd->kd", score_gradient, query_block, preferred_element_type=F32)
            * scale
        )
        value_gradient = jnp.einsum(
            "hqk,hqd->kd", shares.astype(BF16), gradient_block, preferred_element_type=F32
        )
        carry = carry + jnp.concatenate([key_gradient, value_gradient], axis=1)
        return (carry, query_gradient.astype(BF16))

    keyval_sum, query_gradient_blocks = lax.scan(
        back_block,
        jnp.zeros((prompt_total + CONT_DEV, 2 * HD), F32),
        (query_blocks, by_heads(attended_gradient), log_totals),
    )
    query_gradient = by_rows(query_gradient_blocks)
    prompt_part = halve(keyval_sum[:prompt_total].reshape(fsdp, PR_DEV, 2 * HD), "fsdp")[0]
    own_part = jnp.concatenate([prompt_part, keyval_sum[prompt_total:]], axis=0)
    keyval_gradient = ring_scatter(ring_parts(own_part, 0)).astype(BF16)

    query_weight_sum = lax.psum_scatter(
        dot(normed.T, query_gradient).astype(BF16), GF, scatter_dimension=0, tiled=True
    ).astype(F32)
    query_weight_gradient = ring_scatter(ring_parts(query_weight_sum, 1))
    query_shift_gradient = jnp.sum(query_gradient, axis=0, dtype=F32)
    keyval_weight_gradient = dot(normed.T, keyval_gradient)
    value_shift_gradient = jnp.sum(keyval_gradient[:, HD:], axis=0, dtype=F32)
    normed_gradient = dot(query_gradient, query_full.T) + dot(keyval_gradient, keyval_full.T)
    input_part, gain_one_gradient, shift_one_gradient = norm_one_back(normed_gradient)
    input_gradient = (middle_gradient + input_part).astype(BF16)

    upward_slots = jnp.where(
        (jnp.arange(tp) == column)[:, None], upward_shift_gradient[None, :], 0.0
    )
    pieces = [
        keyval_weight_gradient.reshape(shards, -1),
        gain_one_gradient.reshape(shards, -1),
        shift_one_gradient.reshape(shards, -1),
        output_shift_gradient.reshape(shards, -1),
        gain_two_gradient.reshape(shards, -1),
        shift_two_gradient.reshape(shards, -1),
        downward_shift_gradient.reshape(shards, -1),
        query_shift_gradient.reshape(heads, shards, -1).transpose(1, 0, 2).reshape(shards, -1),
        value_shift_gradient.reshape(shards, -1),
        upward_slots.reshape(tp, upward_bias.shape[0], shards, -1)
        .transpose(2, 0, 1, 3)
        .reshape(shards, -1),
    ]
    sizes = [piece.shape[1] for piece in pieces]
    filled = sum(sizes)
    padded = -(-filled // 4096) * 4096
    packed = jnp.concatenate(pieces + [jnp.zeros((shards, padded - filled), F32)], axis=1)
    packed = packed.astype(BF16).reshape(shards, padded // 256, 256)
    packed = jnp.concatenate(
        [lax.dynamic_index_in_dim(packed, owner_of ^ m, 0) for m in range(shards)]
    ).astype(F32)
    packed = total_over(halve(halve(packed, "grp"), "fsdp")[0], "tp").reshape(-1)
    fields = []
    start = 0
    for size in sizes:
        fields.append(packed[start : start + size])
        start += size
    return (
        layer_output,
        input_gradient,
        fields[1],
        fields[2],
        query_weight_gradient,
        lax.dynamic_slice_in_dim(fields[7].reshape(heads, -1), column * heads_local, heads_local),
        fields[0].reshape(-1, 2 * HD),
        fields[8],
        output_gradient,
        fields[3],
        fields[4],
        fields[5],
        upward_gradient,
        lax.dynamic_index_in_dim(
            fields[9].reshape(tp, upward_bias.shape[0], -1), column, 0, keepdims=False
        ),
        downward_gradient,
        fields[6],
    )


def solution(mesh):
    in_specs = (
        P(("grp", "fsdp", "tp"), None),
        P(("grp", "fsdp", "tp"), None),
        P("grp", None),
        P(("grp", "fsdp"), None),
        P(("grp", "fsdp")),
        P(("grp", "fsdp")),
        P(("grp", "fsdp"), "tp"),
        P("tp", ("grp", "fsdp")),
        P(("grp", "fsdp"), None),
        P(("grp", "fsdp")),
        P("tp", ("grp", "fsdp")),
        P(("grp", "fsdp")),
        P(("grp", "fsdp")),
        P(("grp", "fsdp")),
        P(("grp", "fsdp"), "tp"),
        P("tp", ("grp", "fsdp")),
        P("tp", ("grp", "fsdp")),
        P(("grp", "fsdp")),
    )
    out_specs = (
        P(("grp", "fsdp", "tp"), None),
        P(("grp", "fsdp", "tp"), None),
        P(("grp", "fsdp")),
        P(("grp", "fsdp")),
        P(("grp", "fsdp"), "tp"),
        P("tp", ("grp", "fsdp")),
        P(("grp", "fsdp"), None),
        P(("grp", "fsdp")),
        P("tp", ("grp", "fsdp")),
        P(("grp", "fsdp")),
        P(("grp", "fsdp")),
        P(("grp", "fsdp")),
        P(("grp", "fsdp"), "tp"),
        P("tp", ("grp", "fsdp")),
        P("tp", ("grp", "fsdp")),
        P(("grp", "fsdp")),
    )
    return jax.shard_map(
        on_device, mesh=mesh, in_specs=in_specs, out_specs=out_specs, check_vma=False
    )
```

```python
import jax
import jax.numpy as jnp
from jax import lax
from jax.experimental import pallas as pl
from jax.experimental.pallas import tpu as pltpu
from jax.sharding import PartitionSpec as P

HD = 128
PBLK = 128
PB_DEV = 2
CONT_DEV = 768
PR_DEV = 256
ROWS = 1024
HEAD_BLOCK = 4
KEY_BLOCK = 256
LOG_SCALE = HD ** (-0.5) * 1.4426950408889634

EPSILON = 1e-05
MASKED = -1e30
GELU_SLOPE = 0.7978845608028654
GELU_CUBIC = 0.044715
GF = ("grp", "fsdp")
F32 = jnp.float32
BF16 = jnp.bfloat16


def layer_norm(values, gain, shift):
    centre = jnp.mean(values, axis=-1, keepdims=True)
    centred = values - centre
    spread = jnp.mean(centred * centred, axis=-1, keepdims=True)
    return centred * lax.rsqrt(spread + EPSILON) * gain + shift


def gelu_tanh(values):
    return (
        0.5
        * values
        * (1.0 + jnp.tanh(GELU_SLOPE * (values + GELU_CUBIC * values * values * values)))
    )


def contract(left, right, left_dim, right_dim):
    return lax.dot_general(left, right, (((left_dim,), (right_dim,)), ((), ())), preferred_element_type=F32)

def fill_bias(bias_ref, order_query, owner_query, order_key, owner_key):
    allowed = (order_key[...] <= order_query[...]) & (
        (owner_key[...] < 0) | (owner_key[...] == owner_query[...])
    )
    bias_ref[...] = jnp.where(allowed, 0.0, MASKED)

def attend_kernel(order_query, owner_query, order_key, owner_key, query_ref, key_ref, value_ref, out_ref, log_ref, bias_ref, score_ref):
    @pl.when(pl.program_id(0) == 0)
    def _():
        fill_bias(bias_ref, order_query, owner_query, order_key, owner_key)
    spans = [pl.ds(i, KEY_BLOCK) for i in range(0, key_ref.shape[0], KEY_BLOCK)]
    def head(h):
        return pl.ds(h * HD, HD)
    def score(h, span, top):
        part = contract(key_ref[span, :], query_ref[:, head(h)], 1, 1) * LOG_SCALE + bias_ref[span, :]
        score_ref[h % 2, span, :] = part
        part = jnp.max(part, axis=0, keepdims=True)
        return part if top is None else jnp.maximum(top, part)
    top = None
    for span in spans:
        top = score(0, span, top)
    for h in range(HEAD_BLOCK):
        next_top, total, result = None, None, None
        for span in spans:
            weights = jnp.exp2(score_ref[h % 2, span, :] - top)
            part = jnp.sum(weights, axis=0, keepdims=True)
            total = part if total is None else total + part
            part = contract(value_ref[:, span], weights.astype(BF16), 1, 0)
            result = part if result is None else result + part
            if h + 1 < HEAD_BLOCK:
                next_top = score(h + 1, span, next_top)
        out_ref[:, head(h)] = (result / total).T.astype(BF16)
        log_ref[h] = top + jnp.log2(total)
        top = next_top

def attend(queries, keys, values, labels):
    rows, width = queries.shape
    count = keys.shape[0]
    heads = width // HD
    whole = lambda shape: pl.BlockSpec(shape, lambda i: (0,) * len(shape))
    wide = HEAD_BLOCK * HD
    return pl.pallas_call(
        attend_kernel,
        grid=(heads // HEAD_BLOCK,),
        in_specs=[whole((1, rows)), whole((1, rows)), whole((count, 1)), whole((count, 1)),
            pl.BlockSpec((rows, wide), lambda i: (0, i)), whole((count, HD)), whole((HD, count))],
        out_specs=[pl.BlockSpec((rows, wide), lambda i: (0, i)), pl.BlockSpec((HEAD_BLOCK, 1, rows), lambda i: (i, 0, 0))],
        out_shape=[jax.ShapeDtypeStruct((rows, width), BF16), jax.ShapeDtypeStruct((heads, 1, rows), F32)],
        scratch_shapes=[pltpu.VMEM((count, rows), F32), pltpu.VMEM((2, count, rows), F32)],
        cost_estimate=pl.CostEstimate(flops=4 * rows * width * count, bytes_accessed=4 * rows * width + 4 * count * HD, transcendentals=heads * rows * count),
        name="attend",
    )(*labels, queries, keys, values.T)

def back_kernel(order_query, owner_query, order_key, owner_key, query_ref, grad_ref, out_ref, log_ref, key_ref, value_ref, turned_ref,
                query_grad_ref, key_grad_ref, value_grad_ref, bias_ref, share_ref, score_ref):
    @pl.when(pl.program_id(0) == 0)
    def _():
        fill_bias(bias_ref, order_query, owner_query, order_key, owner_key)
        key_grad_ref[...] = jnp.zeros_like(key_grad_ref)
        value_grad_ref[...] = jnp.zeros_like(value_grad_ref)
    rows = query_ref.shape[0]
    spans = [pl.ds(i, KEY_BLOCK) for i in range(0, key_ref.shape[0], KEY_BLOCK)]
    for h in range(HEAD_BLOCK):
        head = pl.ds(h * HD, HD)
        own = pl.ds(h * rows, rows)
        query = query_ref[:, head]
        grad = grad_ref[:, head]
        centre = jnp.sum((grad.astype(F32) * out_ref[:, head].astype(F32)).T, axis=0, keepdims=True)
        log = log_ref[h]
        result = None
        for span in spans:
            shares = jnp.exp2(contract(key_ref[span, :], query, 1, 1) * LOG_SCALE + bias_ref[span, :] - log)
            score_grad = (shares * (contract(value_ref[span, :], grad, 1, 1) - centre)).astype(BF16)
            share_ref[span, own] = shares.astype(BF16)
            score_ref[span, own] = score_grad
            part = contract(turned_ref[:, span], score_grad, 1, 0)
            result = part if result is None else result + part
        query_grad_ref[:, head] = (result * HD ** (-0.5)).T.astype(BF16)
    queries = jnp.concatenate([query_ref[:, pl.ds(h * HD, HD)] for h in range(HEAD_BLOCK)], axis=0)
    grads = jnp.concatenate([grad_ref[:, pl.ds(h * HD, HD)] for h in range(HEAD_BLOCK)], axis=0)
    for span in spans:
        key_grad_ref[span, :] += contract(score_ref[span, :], queries, 1, 0)
        value_grad_ref[span, :] += contract(share_ref[span, :], grads, 1, 0)

def attend_back(queries, grads, attended, logs, keys, values, labels):
    rows, width = queries.shape
    count = keys.shape[0]
    heads = width // HD
    whole = lambda shape: pl.BlockSpec(shape, lambda i: (0,) * len(shape))
    wide = HEAD_BLOCK * HD
    part = pl.BlockSpec((rows, wide), lambda i: (0, i))
    return pl.pallas_call(
        back_kernel,
        grid=(heads // HEAD_BLOCK,),
        in_specs=[whole((1, rows)), whole((1, rows)), whole((count, 1)), whole((count, 1)),
            part, part, part, pl.BlockSpec((HEAD_BLOCK, 1, rows), lambda i: (i, 0, 0)), whole((count, HD)), whole((count, HD)), whole((HD, count))],
        out_specs=[part, whole((count, HD)), whole((count, HD))],
        out_shape=[jax.ShapeDtypeStruct((rows, width), BF16), jax.ShapeDtypeStruct((count, HD), F32), jax.ShapeDtypeStruct((count, HD), F32)],
        scratch_shapes=[pltpu.VMEM((count, rows), F32), pltpu.VMEM((count, HEAD_BLOCK * rows), BF16), pltpu.VMEM((count, HEAD_BLOCK * rows), BF16)],
        cost_estimate=pl.CostEstimate(flops=10 * rows * width * count, bytes_accessed=8 * rows * width + 16 * count * HD, transcendentals=heads * rows * count),
        name="attend_back",
    )(*labels, queries, grads, attended, logs, keys, values, keys.T)

def dot(left, right):
    return jnp.dot(left, right, preferred_element_type=F32)


def shift(values, axis="tp"):
    count = lax.axis_size(axis)
    return lax.ppermute(values, axis, [(i, (i + 1) % count) for i in range(count)])


def flip(values, axis, step):
    count = lax.axis_size(axis)
    return lax.ppermute(values, axis, [(i, i ^ step) for i in range(count)])


def after(values, *others):
    return lax.optimization_barrier((values, *others))[0]


def ring_gather(values):
    blocks = [values]
    for _ in range(lax.axis_size("tp") - 1):
        blocks.append(shift(blocks[-1]))
    return blocks


def ring_place(blocks, axis):
    count = len(blocks)
    me = lax.axis_index("tp")
    width = blocks[0].shape[axis]
    shape = list(blocks[0].shape)
    shape[axis] = width * count
    whole = jnp.zeros(shape, blocks[0].dtype)
    for s, block in enumerate(blocks):
        whole = lax.dynamic_update_slice_in_dim(
            whole, block, lax.rem(me - s + count, count) * width, axis
        )
    return whole


def ring_scatter(parts, beside=()):
    count = len(parts)
    total = parts[1 % count]
    for s in range(1, count):
        came = shift(total.astype(BF16))
        if s <= len(beside):
            came = after(came, beside[s - 1])
        total = came.astype(F32) + parts[(s + 1) % count]
    return total


def ring_parts(values, axis):
    count = lax.axis_size("tp")
    me = lax.axis_index("tp")
    width = values.shape[axis] // count
    return [
        lax.dynamic_slice_in_dim(values, lax.rem(me - s + count, count) * width, width, axis)
        for s in range(count)
    ]


def relative_gather(values):
    blocks = [values]
    for m in range(1, lax.axis_size("fsdp")):
        top = 1 << (m.bit_length() - 1)
        blocks.append(flip(blocks[m ^ top], "fsdp", top))
    return blocks


def halve(values, axis):
    step = lax.axis_size(axis)
    while step > 1:
        step //= 2
        half = values.shape[0] // 2
        values = values[:half] + flip(values[half:].astype(BF16), axis, step).astype(F32)
    return values


def total_over(values, axis):
    step = lax.axis_size(axis)
    while step > 1:
        step //= 2
        values = values + flip(values.astype(BF16), axis, step).astype(F32)
    return values


def exchange_orders():
    steps = [1 << i for i in range(lax.axis_size("fsdp").bit_length() - 1)]
    orders = []
    for side in (steps, steps[::-1]):
        offsets = [0]
        for step in side:
            offsets = offsets + [m ^ step for m in offsets]
        orders.append((side, offsets))
    return orders


def by_distance(values, offsets, apart=None):
    grp = lax.axis_size("grp")
    fsdp = lax.axis_size("fsdp")
    group = lax.axis_index("grp")
    place = lax.axis_index("fsdp")
    size = values.shape[1] // (grp * fsdp)
    parts = [
        lax.dynamic_slice_in_dim(values, ((group ^ a) * fsdp + (place ^ m)) * size, size, 1)
        for a in (range(grp) if apart is None else [apart])
        for m in offsets
    ]
    return jnp.concatenate(parts, axis=1)


def from_distance(values, offsets):
    grp = lax.axis_size("grp")
    fsdp = lax.axis_size("fsdp")
    group = lax.axis_index("grp")
    place = lax.axis_index("fsdp")
    size = values.shape[1] // (grp * fsdp)
    values = jnp.concatenate(
        [
            lax.slice_in_dim(
                values, (a * fsdp + offsets.index(m)) * size, (a * fsdp + offsets.index(m) + 1) * size, axis=1
            )
            for a in range(grp)
            for m in range(fsdp)
        ],
        axis=1,
    )
    return by_distance(values, list(range(fsdp)))


def gather_rows(block):
    half = block.shape[1] // 2
    sides = []
    for side, (steps, _) in enumerate(exchange_orders()):
        sides.append(block[:, side * half : (side + 1) * half])
    for round_ in range(len(exchange_orders()[0][0])):
        for side, (steps, _) in enumerate(exchange_orders()):
            sides[side] = jnp.concatenate(
                [sides[side], flip(sides[side], "fsdp", steps[round_])], axis=0
            )
    return [
        [stack] + [flip(stack, "grp", a) for a in range(1, lax.axis_size("grp"))]
        for stack in sides
    ]


def scatter_begin(left, right):
    assert lax.axis_size("grp") == 2
    half = right.shape[1] // 2
    sides = []
    for side, (_, offsets) in enumerate(exchange_orders()):
        part = right[:, side * half : (side + 1) * half]
        away = dot(by_distance(left, offsets, 1).T, part).astype(BF16)
        kept = dot(by_distance(left, offsets, 0).T, part)
        sides.append((kept + flip(away, "grp", 1).astype(F32)).astype(BF16))
    return sides


def scatter_end(sides, beside=()):
    orders = exchange_orders()
    count = len(orders[0][0])
    sides = list(sides)
    for round_ in range(count):
        for side, (steps, _) in enumerate(orders):
            half = sides[side].shape[0] // 2
            came = flip(sides[side][half:], "fsdp", steps[count - 1 - round_])
            if round_ < len(beside):
                came = after(came, beside[round_])
            sides[side] = (sides[side][:half].astype(F32) + came.astype(F32)).astype(BF16)
    return jnp.concatenate(sides, axis=1).astype(F32)


def on_device(
    layer_input,
    cotangent,
    prompt_blocks,
    cont_lengths,
    first_gain,
    first_shift,
    query_weight,
    query_bias,
    keyval_weight,
    value_bias,
    output_weight,
    output_bias,
    second_gain,
    second_shift,
    upward_weight,
    upward_bias,
    downward_weight,
    downward_bias,
):
    tp = lax.axis_size("tp")
    fsdp = lax.axis_size("fsdp")
    shards = lax.axis_size("grp") * fsdp
    place = lax.axis_index("fsdp")
    column = lax.axis_index("tp")
    owner_of = lax.axis_index("grp") * fsdp + place
    local_count, width = layer_input.shape
    heads_local = query_bias.shape[0]
    heads = heads_local * tp
    scale = HD ** (-0.5)

    query_rows = ring_place(ring_gather(query_weight), 1)
    output_rows = ring_place(ring_gather(after(output_weight, query_rows)), 0)

    pieces = [
        first_gain,
        first_shift,
        output_bias,
        second_gain,
        second_shift,
        downward_bias,
        query_bias.reshape(-1),
        value_bias,
        upward_bias.reshape(-1),
    ]
    sizes = [piece.shape[0] for piece in pieces]
    filled = sum(sizes)
    padded = -(-filled // 4096) * 4096
    packed = jnp.concatenate(pieces + [jnp.zeros((padded - filled,), BF16)]).reshape(-1, 2 * HD)
    packed = jnp.concatenate([keyval_weight, packed], axis=0)
    packed = lax.all_gather(packed, GF, axis=0)
    keyval_rows = keyval_weight.shape[0]
    keyval_full = packed[:, :keyval_rows].reshape(width, 2 * HD)
    packed = packed[:, keyval_rows:].reshape(shards, padded)
    fields = [None]
    start = 0
    for size in sizes:
        fields.append(packed[:, start : start + size])
        start += size
    gain_one, shift_one, output_shift, gain_two, shift_two, downward_shift = (
        field.reshape(-1).astype(F32) for field in fields[1:7]
    )
    query_shift = (
        fields[7].reshape(shards, heads_local, -1).transpose(1, 0, 2).reshape(heads_local * HD)
    )
    query_shift = ring_place(ring_gather(query_shift), 0).astype(F32)
    value_shift = fields[8].reshape(-1).astype(F32)
    upward_shift = (
        fields[9]
        .reshape(shards, upward_bias.shape[0], -1)
        .transpose(1, 0, 2)
        .reshape(-1)
        .astype(F32)
    )

    query_sides = gather_rows(query_rows)
    output_full = lax.all_gather(output_rows, GF, axis=1, tiled=True)

    blocks = prompt_blocks[0]
    prompt_total = blocks.shape[0] * PBLK
    offsets = jnp.arange(PBLK, dtype=jnp.int32)

    def order_of(spot):
        mine = lax.dynamic_slice_in_dim(blocks, spot * PB_DEV, PB_DEV)
        return (mine[:, None] * PBLK + offsets[None, :]).reshape(-1)

    prompt_order = jnp.concatenate([order_of(place ^ m) for m in range(fsdp)])
    spots = jnp.arange(CONT_DEV, dtype=jnp.int32)
    ends = jnp.cumsum(cont_lengths[0])
    segment = jnp.sum((spots[:, None] >= ends[None, :]).astype(jnp.int32), axis=1)
    cont_order = prompt_total + spots
    order_key = jnp.concatenate([prompt_order, cont_order])
    owner_key = jnp.concatenate([jnp.full((prompt_total,), -1, jnp.int32), segment])
    order_rows = jnp.concatenate([order_of(place), cont_order])
    owner_rows = jnp.concatenate([jnp.full((PR_DEV,), -1, jnp.int32), segment])
    order_query = lax.dynamic_slice_in_dim(order_rows, column * local_count, local_count)
    owner_query = lax.dynamic_slice_in_dim(owner_rows, column * local_count, local_count)
    labels = (order_query[None, :], owner_query[None, :], order_key[:, None], owner_key[:, None])

    local_rows = layer_input.astype(F32)
    normed_wide, norm_one_back = jax.vjp(layer_norm, local_rows, gain_one, shift_one)
    normed = normed_wide.astype(BF16)
    value_pad = jnp.concatenate([jnp.zeros((HD,), F32), value_shift])
    keyval = (dot(normed, keyval_full) + value_pad).astype(BF16)
    place_keyval = ring_place(ring_gather(keyval), 0)
    all_keyval = jnp.concatenate(
        relative_gather(place_keyval[:PR_DEV]) + [place_keyval[PR_DEV:]], axis=0
    )
    keys = all_keyval[:, :HD]
    values = all_keyval[:, HD:]
    half = heads * HD // 2
    group_width = width // lax.axis_size("grp")
    queries = []
    for (_, offsets), stacks in zip(exchange_orders(), query_sides):
        queries.append(
            sum(dot(by_distance(normed, offsets, a), stack) for a, stack in enumerate(stacks))
        )
    queries = (jnp.concatenate(queries, axis=1) + query_shift).astype(BF16)
    upward_full = lax.all_gather(after(upward_weight, queries), GF, axis=0, tiled=True)
    cotangent_blocks = ring_gather(after(cotangent, all_keyval))
    attended, log_totals = attend(queries, keys, values, labels)
    downward_full = lax.all_gather(after(downward_weight, attended), GF, axis=1, tiled=True)
    middle = local_rows + dot(attended, output_full) + output_shift
    normed_two_wide, norm_two_back = jax.vjp(layer_norm, middle, gain_two, shift_two)
    normed_two_blocks = ring_gather(normed_two_wide.astype(BF16))

    feed_parts = []
    back_parts = []
    active_blocks = []
    hidden_gradient_blocks = []
    for block, upstream_block in zip(normed_two_blocks, cotangent_blocks):
        hidden = dot(block, upward_full) + upward_shift
        active_wide, gelu_back = jax.vjp(gelu_tanh, hidden)
        active = active_wide.astype(BF16)
        active_gradient = dot(upstream_block, downward_full.T)
        hidden_gradient = gelu_back(active_gradient)[0].astype(BF16)
        active_blocks.append(active)
        hidden_gradient_blocks.append(hidden_gradient)
        back_parts.append(dot(hidden_gradient, upward_full.T))
        feed_parts.append(dot(active, downward_full))
    upstream = cotangent.astype(F32)
    active_rows = jnp.concatenate(active_blocks, axis=0)
    upstream_rows = jnp.concatenate(cotangent_blocks, axis=0)
    normed_two_rows = jnp.concatenate(normed_two_blocks, axis=0)
    hidden_gradient_rows = jnp.concatenate(hidden_gradient_blocks, axis=0)
    downward_product = dot(active_rows.T, upstream_rows).astype(BF16)
    upward_product = dot(normed_two_rows.T, hidden_gradient_rows).astype(BF16)
    normed_two_gradient = ring_scatter(back_parts, [downward_product, upward_product])
    downward_gradient = lax.psum_scatter(
        downward_product, GF, scatter_dimension=1, tiled=True
    ).astype(F32)
    upward_gradient = lax.psum_scatter(
        upward_product, GF, scatter_dimension=0, tiled=True
    ).astype(F32)
    upward_shift_gradient = jnp.sum(hidden_gradient_rows, axis=0, dtype=F32)
    downward_shift_gradient = jnp.sum(upstream, axis=0)

    middle_part, gain_two_gradient, shift_two_gradient = norm_two_back(normed_two_gradient)
    middle_gradient = upstream + middle_part
    output_shift_gradient = jnp.sum(middle_gradient, axis=0)
    mixed_gradient = middle_gradient.astype(BF16)
    attended_gradient = dot(mixed_gradient, output_full.T).astype(BF16)
    output_sides = scatter_begin(mixed_gradient, attended)
    attended_gradient = lax.optimization_barrier((attended_gradient, output_sides))[0]
    query_gradient, key_sum, value_sum = attend_back(
        queries, attended_gradient, attended, log_totals, keys, values, labels
    )
    keyval_sum = jnp.concatenate([key_sum * scale, value_sum], axis=1)
    prompt_part = halve(keyval_sum[:prompt_total].reshape(fsdp, PR_DEV, 2 * HD), "fsdp")[0]
    own_part = jnp.concatenate([prompt_part, keyval_sum[prompt_total:]], axis=0)
    keyval_gradient = ring_scatter(ring_parts(own_part, 0)).astype(BF16)

    output_sum = scatter_end(output_sides, [query_gradient])
    output_gradient = ring_scatter(ring_parts(output_sum, 1)).T
    query_sides_gradient = scatter_begin(normed, query_gradient)
    query_weight_sum = scatter_end(query_sides_gradient)
    query_weight_gradient = ring_scatter(ring_parts(query_weight_sum, 1))
    query_shift_gradient = jnp.sum(query_gradient, axis=0, dtype=F32)
    keyval_weight_gradient = dot(normed.T, keyval_gradient)
    value_shift_gradient = jnp.sum(keyval_gradient[:, HD:], axis=0, dtype=F32)
    late_gradient = lax.optimization_barrier((query_gradient, query_sides_gradient))[0]
    normed_gradient = dot(keyval_gradient, keyval_full.T)
    for side, ((_, offsets), stacks) in enumerate(zip(exchange_orders(), query_sides)):
        part = late_gradient[:, side * half : (side + 1) * half]
        normed_gradient = normed_gradient + from_distance(
            jnp.concatenate([dot(part, stack.T) for stack in stacks], axis=1), offsets
        )
    feed_parts = lax.optimization_barrier((feed_parts, normed_two_gradient))[0]
    fed = ring_scatter(feed_parts, [attended_gradient, query_gradient])
    layer_output = (middle + fed + downward_shift).astype(BF16)
    input_part, gain_one_gradient, shift_one_gradient = norm_one_back(normed_gradient)
    input_gradient = (middle_gradient + input_part).astype(BF16)

    upward_slots = jnp.where(
        (jnp.arange(tp) == column)[:, None], upward_shift_gradient[None, :], 0.0
    )
    pieces = [
        gain_one_gradient.reshape(shards, -1),
        shift_one_gradient.reshape(shards, -1),
        output_shift_gradient.reshape(shards, -1),
        gain_two_gradient.reshape(shards, -1),
        shift_two_gradient.reshape(shards, -1),
        downward_shift_gradient.reshape(shards, -1),
        query_shift_gradient.reshape(heads, shards, -1).transpose(1, 0, 2).reshape(shards, -1),
        value_shift_gradient.reshape(shards, -1),
        upward_slots.reshape(tp, upward_bias.shape[0], shards, -1)
        .transpose(2, 0, 1, 3)
        .reshape(shards, -1),
    ]
    sizes = [piece.shape[1] for piece in pieces]
    filled = sum(sizes)
    padded = -(-filled // 4096) * 4096
    packed = jnp.concatenate(pieces + [jnp.zeros((shards, padded - filled), F32)], axis=1)
    packed = jnp.concatenate(
        [
            keyval_weight_gradient.astype(BF16).reshape(shards, -1, 2 * HD),
            packed.astype(BF16).reshape(shards, padded // 256, 256),
        ],
        axis=1,
    )
    packed = jnp.concatenate(
        [lax.dynamic_index_in_dim(packed, owner_of ^ m, 0) for m in range(shards)]
    ).astype(F32)
    packed = total_over(halve(halve(packed, "grp"), "fsdp")[0], "tp")
    keyval_weight_gradient = packed[:keyval_rows]
    packed = packed[keyval_rows:].reshape(-1)
    fields = [None]
    start = 0
    for size in sizes:
        fields.append(packed[start : start + size])
        start += size
    return (
        layer_output,
        input_gradient,
        fields[1],
        fields[2],
        query_weight_gradient,
        lax.dynamic_slice_in_dim(fields[7].reshape(heads, -1), column * heads_local, heads_local),
        keyval_weight_gradient,
        fields[8],
        output_gradient,
        fields[3],
        fields[4],
        fields[5],
        upward_gradient,
        lax.dynamic_index_in_dim(
            fields[9].reshape(tp, upward_bias.shape[0], -1), column, 0, keepdims=False
        ),
        downward_gradient,
        fields[6],
    )


def solution(mesh):
    in_specs = (
        P(("grp", "fsdp", "tp"), None),
        P(("grp", "fsdp", "tp"), None),
        P("grp", None),
        P(("grp", "fsdp"), None),
        P(("grp", "fsdp")),
        P(("grp", "fsdp")),
        P(("grp", "fsdp"), "tp"),
        P("tp", ("grp", "fsdp")),
        P(("grp", "fsdp"), None),
        P(("grp", "fsdp")),
        P("tp", ("grp", "fsdp")),
        P(("grp", "fsdp")),
        P(("grp", "fsdp")),
        P(("grp", "fsdp")),
        P(("grp", "fsdp"), "tp"),
        P("tp", ("grp", "fsdp")),
        P("tp", ("grp", "fsdp")),
        P(("grp", "fsdp")),
    )
    out_specs = (
        P(("grp", "fsdp", "tp"), None),
        P(("grp", "fsdp", "tp"), None),
        P(("grp", "fsdp")),
        P(("grp", "fsdp")),
        P(("grp", "fsdp"), "tp"),
        P("tp", ("grp", "fsdp")),
        P(("grp", "fsdp"), None),
        P(("grp", "fsdp")),
        P("tp", ("grp", "fsdp")),
        P(("grp", "fsdp")),
        P(("grp", "fsdp")),
        P(("grp", "fsdp")),
        P(("grp", "fsdp"), "tp"),
        P("tp", ("grp", "fsdp")),
        P("tp", ("grp", "fsdp")),
        P(("grp", "fsdp")),
    )
    return jax.shard_map(
        on_device, mesh=mesh, in_specs=in_specs, out_specs=out_specs, check_vma=False
    )
```
